32 devices in a mesh: groups: 2 (over x), ctx: 8 (over z, y), head: 2 (over core).
Axes of the slice: x: 2, y: 2, z: 4, core: 2. Of those that a mesh axis runs over, the one named last changes fastest.
Arguments:
- queries: bfloat16 [2, 256, 64, 128], P('groups', 'ctx', 'head'), parts along dimension 0, may hold values from -400 to 400
- new_keys: bfloat16 [2, 256, 8, 128], P('groups', 'ctx', 'head'), parts along dimension 0, may hold values from -5 to 5
- new_values: bfloat16 [2, 256, 8, 128], P('groups', 'ctx', 'head'), parts along dimension 0, may hold values from -6 to 6
- history_keys: bfloat16 [2, 8192, 8, 128], P('groups', 'ctx', 'head'), parts along dimension 0, may hold values from -6 to 6
- history_values: bfloat16 [2, 8192, 8, 128], P('groups', 'ctx', 'head'), parts along dimension 0, may hold values from -6 to 6
- block_mask: int32 [2, 2, 64], P('groups', None, 'ctx'), parts along dimension 0, may hold values from 0 to 1, as said below
Outputs:
- attended: bfloat16 [2, 256, 64, 128], P('groups', 'ctx', 'head'), parts along dimension 0
The draws below stay inside these ranges and needn't reach their ends.
There are 2 independent parts, one for each index of `groups`. The reference program is written for one: setup_inputs(seed, part) draws one part's arguments, and reference() takes and returns one part's arrays. A program takes and returns all parts, laid end to end along the dimension named above; each array names one. Nothing has to cross between parts.
Inputs may be any that keep to these rules, and one draw needn't show every extreme that they name: `block_mask`: 0 or 1 for each pair of a block of 128 new tokens and a block of 128 history positions of the same session.
All inputs are finite; a program needn't handle non-finite values.
Results may differ from the reference program's by a relative error of at most 0.0013.
Values may be sent and summed in bfloat16 or wider, within the bound.
A program may use at most 64 MiB of HBM per device.

```python
import math
import jax
import jax.numpy as jnp
from jax import lax

QH = 64
KVH = 8
HD = 128
BLK = 128
SESS = 1
NEW = 256
CTX = 8192
QB = 2
HB = 64
HB_DEV = 8


def drawn_pair(key):
    base = jax.random.fold_in(key, 11)
    first_key, second_key = jax.random.split(base)
    keys_new = jnp.clip(jax.random.normal(first_key, (SESS, NEW, KVH, HD), jnp.float32), -5.0, 5.0)
    query_rows = jnp.clip(jax.random.normal(second_key, (SESS, NEW, QH, HD), jnp.float32), -5.0, 5.0)
    return (query_rows, keys_new)


def draw_queries(key, part):
    return drawn_pair(key)[0].astype(jnp.bfloat16)


def draw_new_keys(key, part):
    return drawn_pair(key)[1].astype(jnp.bfloat16)


def draw_block_mask(key, part):
    level_key, bits_key, row_key, col_key = jax.random.split(jax.random.fold_in(key, 23), 4)
    owners = HB // HB_DEV
    level = jax.random.randint(level_key, (SESS, 1, owners), 1, 4)
    level_full = jnp.repeat(level, HB_DEV, axis=2)
    bits = jax.random.randint(bits_key, (SESS, QB, HB), 0, 16)
    live = bits < level_full
    pick_row = jax.random.randint(row_key, (SESS, owners), 0, QB)
    pick_col = jax.random.randint(col_key, (SESS, owners), 0, HB_DEV)
    row_full = jnp.repeat(pick_row, HB_DEV, axis=1)[:, None, :]
    col_full = jnp.repeat(pick_col, HB_DEV, axis=1)[:, None, :]
    blocks = jnp.arange(HB)[None, None, :]
    rows = jnp.arange(QB)[None, :, None]
    forced = (rows == row_full) & (blocks % HB_DEV == col_full)
    return (live | forced).astype(jnp.int32)


def level_of(stream_key, shape, shards, smallest, top_value):
    def one(dim, blocks):
        draws = jax.random.uniform(jax.random.fold_in(jax.random.fold_in(stream_key, 6), dim), (blocks,), jnp.float32, smallest / len(shards), top_value / len(shards))
        return jnp.repeat(jnp.exp(draws), shape[dim] // blocks).reshape((-1,) + (1,) * (len(shape) - dim - 1))

    loudness = one(*shards[0])
    for cut in shards[1:]:
        loudness = loudness * one(*cut)
    return loudness


def gaussian(key, extent, spread, bound, cuts=(), held_as=jnp.bfloat16):
    entries = jax.random.normal(key, extent, jnp.float32) * spread
    if len(cuts) > 0:
        entries = level_of(key, extent, cuts, -0.22, 0.18) * entries
    return jnp.clip(entries, min=-bound, max=bound).astype(held_as)


def setup_inputs(seed: int = 0, part: int = 0) -> dict:
    keys = jax.random.split(jax.random.key(seed), 7)
    own_keys = jax.random.split(jax.random.fold_in(keys[6], part), 7)
    queries = draw_queries(jax.random.fold_in(jax.random.fold_in(keys[6], part), 71), part)
    new_keys = draw_new_keys(jax.random.fold_in(jax.random.fold_in(keys[6], part), 71), part)
    new_values = gaussian(own_keys[2], (SESS, NEW, KVH, HD), 1.0, 6.0, ((1, 8), (2, 2)))
    history_keys = gaussian(own_keys[3], (SESS, CTX, KVH, HD), 1.0, 6.0, ((1, 8), (2, 2)))
    history_values = gaussian(own_keys[4], (SESS, CTX, KVH, HD), 1.0, 6.0, ((1, 8), (2, 2)))
    block_mask = draw_block_mask(jax.random.fold_in(jax.random.fold_in(keys[6], part), 71), part)
    return dict(queries=queries, new_keys=new_keys, new_values=new_values, history_keys=history_keys, history_values=history_values, block_mask=block_mask)


NEG = -1e+30

def reference(queries, new_keys, new_values, history_keys, history_values, block_mask):
    scale = 1.0 / math.sqrt(HD)
    group = QH // KVH
    positions = jnp.arange(NEW, dtype=jnp.int32)
    causal = positions[None, :] <= positions[:, None]

    def one_session(operands):
        query_rows, keys_new, values_new, keys_old, values_old, mask_rows = operands
        live = jnp.repeat(jnp.repeat(mask_rows, BLK, axis=0), BLK, axis=1) > 0
        visible = jnp.concatenate([live, causal], axis=1)
        keys_all = jnp.concatenate([keys_old, keys_new], axis=0).astype(jnp.float32)
        values_all = jnp.concatenate([values_old, values_new], axis=0).astype(jnp.float32)
        grouped = jnp.moveaxis(query_rows.reshape(NEW, KVH, group, HD), 1, 0).astype(jnp.float32)

        def one_head(head_ops):
            q_head, k_head, v_head = head_ops
            scores = jnp.einsum('rgd,cd->grc', q_head, k_head, precision=lax.Precision.HIGHEST) * scale
            masked = jnp.where(visible[None], scores, NEG)
            peak = lax.optimization_barrier(jnp.max(masked, axis=-1, keepdims=True))
            expo = jnp.where(visible[None], jnp.exp(masked - peak), 0.0)
            numer = jnp.einsum('grc,cd->grd', expo, v_head, precision=lax.Precision.HIGHEST)
            return numer / lax.optimization_barrier(jnp.sum(expo, axis=-1))[..., None]
        heads = lax.map(one_head, (grouped, jnp.moveaxis(keys_all, 1, 0), jnp.moveaxis(values_all, 1, 0)))
        return jnp.transpose(heads, (2, 0, 1, 3)).reshape(NEW, QH, HD)
    result = lax.map(one_session, (queries, new_keys, new_values, history_keys, history_values, block_mask))
    return result.astype(jnp.bfloat16)
```

```python
import functools
import math

import jax
import jax.numpy as jnp
from jax import lax
from jax.experimental import pallas as pl
from jax.experimental.pallas import tpu as pltpu
from jax.sharding import PartitionSpec as P

BLK = 128
NEG = -1e30
TINY = 1e-30
TOP = 32767.0
F32 = jnp.float32
BF16 = jnp.bfloat16


def scores_of(q, k):
    return lax.dot_general(q, k, (((1,), (1,)), ((), ())), preferred_element_type=F32)


def weighted(p, v):
    hi = p.astype(BF16)
    lo = (p - hi.astype(F32)).astype(BF16)
    wide = jnp.concatenate([v, jnp.ones_like(v)], axis=1)
    return jnp.dot(hi, wide, preferred_element_type=F32) + jnp.dot(
        lo, wide, preferred_element_type=F32
    )


def compact(x, eye):
    rows = x.shape[0]
    size = eye.shape[0]
    parts = []
    for at in range(0, rows, size):
        piece = jnp.where(eye, x[at : at + size], 0.0)
        parts.append(jnp.sum(piece, axis=0, keepdims=True)[:, :size])
    return parts[0] if len(parts) == 1 else jnp.concatenate(parts, axis=1)


def eye_of(size):
    return lax.broadcasted_iota(jnp.int32, (size, 128), 0) == lax.broadcasted_iota(
        jnp.int32, (size, 128), 1
    )


def hist_kernel(mask_ref, q_ref, k_ref, v_ref, o_ref, st_ref, acc_ref, m_ref):
    chunks, _, rows, hd = q_ref.shape
    b = pl.program_id(1)
    scale = 1.0 / math.sqrt(hd)
    blocks = k_ref.shape[0] // BLK
    acc_ref[...] = jnp.zeros_like(acc_ref)
    m_ref[...] = jnp.full_like(m_ref, NEG)

    @pl.loop(0, blocks)
    def _(j):
        @pl.when(mask_ref[b, j] > 0)
        def _():
            at = pl.ds(pl.multiple_of(j * BLK, BLK), BLK)
            k = k_ref[at, :]
            v = v_ref[at, :]
            for c in range(chunks):
                s = scores_of(q_ref[c, 0], k) * scale
                old = m_ref[c]
                new = jnp.maximum(old, jnp.max(s, axis=1, keepdims=True))
                alpha = jnp.exp(old - new)
                p = jnp.exp(s - new)
                m_ref[c] = new
                acc_ref[c] = acc_ref[c] * jnp.concatenate([alpha, alpha], axis=1) + weighted(p, v)

    eye = eye_of(min(rows, 128))
    for c in range(chunks):
        acc = acc_ref[c]
        num = acc[:, :hd]
        big = jnp.maximum(jnp.max(jnp.abs(num), axis=1, keepdims=True), TINY)
        o_ref[c, 0] = jnp.floor(num * (TOP / big) + 0.5).astype(jnp.int32).astype(jnp.int16)
        st_ref[c, 0, 0:1] = compact(m_ref[c], eye)
        st_ref[c, 0, 1:2] = compact(acc[:, hd:], eye)
        st_ref[c, 0, 2:3] = compact(jnp.broadcast_to(big * (1.0 / TOP), (rows, hd)), eye)
        st_ref[c, 0, 3:8] = jnp.zeros((5, rows), F32)


def new_part(first, q, k, v, group):
    rows, hd = q.shape
    cols = k.shape[0]
    s = scores_of(q, k) * (1.0 / math.sqrt(hd))
    row = first + lax.broadcasted_iota(jnp.int32, (rows, cols), 0) // group
    seen = lax.broadcasted_iota(jnp.int32, (rows, cols), 1) <= row
    s = jnp.where(seen, s, NEG)
    peak = jnp.max(s, axis=1, keepdims=True)
    p = jnp.where(seen, jnp.exp(s - peak), 0.0)
    return jnp.broadcast_to(peak, (rows, hd)), weighted(p, v)


def merged(stats, partial, peak, acc):
    n = len(stats)
    rows, hd = peak.shape
    tops = stats[0][0:1]
    for st in stats[1:]:
        tops = jnp.maximum(tops, st[0:1])
    total = jnp.zeros_like(tops)
    lines = []
    for st in stats:
        w = jnp.exp(st[0:1] - tops)
        total = total + st[1:2] * w
        lines.append(st[2:3] * w)
    lines += [tops, total] + [jnp.zeros_like(tops)] * (-(n + 2) % 8)
    table = jnp.concatenate(lines, axis=0)
    outs = []
    size = min(rows, 128)
    for at in range(0, rows, size):
        cols = jnp.transpose(table[:, at : at + size])
        hist = jnp.zeros((size, hd), F32)
        for d in range(n):
            hist = hist + cols[:, d : d + 1] * partial(d, at, size).astype(jnp.int32).astype(F32)
        mh = cols[:, n : n + 1]
        mn = peak[at : at + size]
        best = jnp.maximum(mh, mn)
        eh = jnp.exp(mh - best)
        en = jnp.exp(mn - best)
        num = eh * hist + en * acc[at : at + size, :hd]
        den = eh * cols[:, n + 1 : n + 2] + en * acc[at : at + size, hd:]
        outs.append(num / den)
    return outs[0] if len(outs) == 1 else jnp.concatenate(outs, axis=0)


def combine_kernel(n, own, q_ref, k_ref, v_ref, o_ref, st_ref, out_ref):
    rows, hd = q_ref.shape[1:]
    first = lax.axis_index("ctx") * own
    peak, acc = new_part(first, q_ref[0], k_ref[...], v_ref[...], rows // own)
    stats = [st_ref[d, 0] for d in range(n)]
    out = merged(stats, lambda d, at, size: o_ref[d, 0, at : at + size], peak, acc)
    out_ref[0] = out.astype(BF16)


def per_device(queries, new_keys, new_values, history_keys, history_values, block_mask):
    _, own, heads, hd = queries.shape
    kv = new_keys.shape[2]
    group = heads // kv
    rows = own * group
    context = history_keys.shape[1]
    n = lax.axis_size("ctx")
    qblocks = block_mask.shape[1]
    chunks = BLK // own

    q = jnp.transpose(queries.reshape(own, kv, group, hd), (1, 0, 2, 3)).reshape(kv, rows, hd)
    q_all = lax.all_gather(q, "ctx", axis=0)
    k_new = lax.all_gather(new_keys.reshape(own, kv * hd), "ctx", axis=0, tiled=True)
    v_new = lax.all_gather(new_values.reshape(own, kv * hd), "ctx", axis=0, tiled=True)
    k_old = history_keys.reshape(context, kv * hd)
    v_old = history_values.reshape(context, kv * hd)

    part, stats = pl.pallas_call(
        hist_kernel,
        grid_spec=pltpu.PrefetchScalarGridSpec(
            num_scalar_prefetch=1,
            grid=(kv, qblocks),
            in_specs=[
                pl.BlockSpec((chunks, 1, rows, hd), lambda g, b, m: (b, g, 0, 0)),
                pl.BlockSpec((context, hd), lambda g, b, m: (0, g)),
                pl.BlockSpec((context, hd), lambda g, b, m: (0, g)),
            ],
            out_specs=[
                pl.BlockSpec((chunks, 1, rows, hd), lambda g, b, m: (b, g, 0, 0)),
                pl.BlockSpec((chunks, 1, 8, rows), lambda g, b, m: (b, g, 0, 0)),
            ],
            scratch_shapes=[
                pltpu.VMEM((chunks, rows, 2 * hd), F32),
                pltpu.VMEM((chunks, rows, hd), F32),
            ],
        ),
        out_shape=[
            jax.ShapeDtypeStruct((n, kv, rows, hd), jnp.int16),
            jax.ShapeDtypeStruct((n, kv, 8, rows), F32),
        ],
        name="hist",
    )(block_mask[0], q_all, k_old, v_old)

    part = lax.all_to_all(part, "ctx", split_axis=0, concat_axis=0, tiled=True)
    stats = lax.all_to_all(stats, "ctx", split_axis=0, concat_axis=0, tiled=True)

    out = pl.pallas_call(
        functools.partial(combine_kernel, n, own),
        grid=(kv,),
        in_specs=[
            pl.BlockSpec((1, rows, hd), lambda g: (g, 0, 0)),
            pl.BlockSpec((n * own, hd), lambda g: (0, g)),
            pl.BlockSpec((n * own, hd), lambda g: (0, g)),
            pl.BlockSpec((n, 1, rows, hd), lambda g: (0, g, 0, 0)),
            pl.BlockSpec((n, 1, 8, rows), lambda g: (0, g, 0, 0)),
        ],
        out_specs=pl.BlockSpec((1, rows, hd), lambda g: (g, 0, 0)),
        out_shape=jax.ShapeDtypeStruct((kv, rows, hd), BF16),
        name="combine",
    )(q, k_new, v_new, part, stats)
    out = jnp.transpose(out.reshape(kv, own, group, hd), (1, 0, 2, 3))
    return out.reshape(1, own, heads, hd)


def solution(mesh):
    spec = P("groups", "ctx", "head", None)
    return jax.shard_map(
        per_device,
        mesh=mesh,
        in_specs=(spec,) * 5 + (P("groups", None, "ctx"),),
        out_specs=spec,
        check_vma=False,
    )
```

```python
import functools
import math

import jax
import jax.numpy as jnp
from jax import lax
from jax.experimental import pallas as pl
from jax.experimental.pallas import tpu as pltpu
from jax.sharding import PartitionSpec as P

BLK = 128
NEG = -1e30
TINY = 1e-30
TOP = 32767.0
F32 = jnp.float32
BF16 = jnp.bfloat16


def scores_of(q, k):
    return lax.dot_general(q, k, (((1,), (1,)), ((), ())), preferred_element_type=F32)


def weighted(p, v):
    hi = p.astype(BF16)
    lo = (p - hi.astype(F32)).astype(BF16)
    wide = jnp.concatenate([v, jnp.ones_like(v)], axis=1)
    return jnp.dot(hi, wide, preferred_element_type=F32) + jnp.dot(
        lo, wide, preferred_element_type=F32
    )


def compact(x, eye):
    rows = x.shape[0]
    size = eye.shape[0]
    parts = []
    for at in range(0, rows, size):
        piece = jnp.where(eye, x[at : at + size], 0.0)
        parts.append(jnp.sum(piece, axis=0, keepdims=True)[:, :size])
    return parts[0] if len(parts) == 1 else jnp.concatenate(parts, axis=1)


def eye_of(size):
    return lax.broadcasted_iota(jnp.int32, (size, 128), 0) == lax.broadcasted_iota(
        jnp.int32, (size, 128), 1
    )


def fold(s, v, acc_ref, m_ref, c, seen=None):
    if seen is not None:
        s = jnp.where(seen, s, NEG)
    old = m_ref[c]
    new = jnp.maximum(old, jnp.max(s, axis=1, keepdims=True))
    alpha = jnp.exp(old - new)
    p = jnp.exp(s - new[:, : s.shape[1]])
    if seen is not None:
        p = jnp.where(seen, p, 0.0)
    m_ref[c] = new
    acc_ref[c] = acc_ref[c] * jnp.concatenate([alpha, alpha], axis=1) + weighted(p, v)


def fixed(num):
    big = jnp.maximum(jnp.max(jnp.abs(num), axis=1, keepdims=True), TINY)
    coded = jnp.floor(num * (TOP / big) + 0.5).astype(jnp.int32).astype(jnp.int16)
    return coded, jnp.broadcast_to(big * (1.0 / TOP), num.shape)


def hist_kernel(kv, own, mask_ref, q_ref, k_ref, v_ref, kn_ref, vn_ref, o_ref, st_ref, acc_ref, m_ref):
    chunks, _, rows, hd = q_ref.shape
    b, g = pl.program_id(0), pl.program_id(1)
    me = lax.axis_index("ctx")
    scale = 1.0 / math.sqrt(hd)
    blocks = k_ref.shape[0] // BLK
    acc_ref[...] = jnp.zeros_like(acc_ref)
    m_ref[...] = jnp.full_like(m_ref, NEG)

    for c in range(chunks):

        @pl.when(b * chunks + c >= me)
        def _():
            s = scores_of(q_ref[c, 0], kn_ref[...]) * scale
            row = (b * chunks + c) * own + lax.broadcasted_iota(
                jnp.int32, (rows, own), 0
            ) // (rows // own)
            seen = me * own + lax.broadcasted_iota(jnp.int32, (rows, own), 1) <= row
            fold(s, vn_ref[...], acc_ref, m_ref, c, seen)

    @pl.loop(0, blocks)
    def _(j):
        @pl.when(mask_ref[b, j] > 0)
        def _():
            at = pl.ds(pl.multiple_of(j * BLK, BLK), BLK)
            k = k_ref[at, :]
            v = v_ref[at, :]
            for c in range(chunks):
                fold(scores_of(q_ref[c, 0], k) * scale, v, acc_ref, m_ref, c)

    eye = eye_of(min(rows, 128))
    for c in range(chunks):
        acc = acc_ref[c]
        coded, step = fixed(acc[:, :hd])
        o_ref[c, 0] = coded
        st_ref[c, pl.ds(g, 1)] = compact(m_ref[c], eye)
        st_ref[c, pl.ds(kv + g, 1)] = compact(acc[:, hd:], eye)
        st_ref[c, pl.ds(2 * kv + g, 1)] = compact(step, eye)


def remote(src, dst, send, recv, where):
    return pltpu.make_async_remote_copy(
        src_ref=src,
        dst_ref=dst,
        send_sem=send,
        recv_sem=recv,
        device_id={"ctx": where},
        device_id_type=pl.DeviceIdType.MESH,
    )


def places(n):
    far = n // 2
    me = lax.axis_index("ctx")
    z, y = me // 2, me % 2
    order = sorted(range(1, far), key=lambda d: abs(2 * d - far))
    ahead = [((z + d) % far) * 2 for d in range(far)]
    behind = [((z + far - d) % far) * 2 for d in range(far)]
    return far, me, y, order, ahead, behind


def meet(far, y, ahead):
    barrier = pltpu.get_barrier_semaphore()
    for where in [ahead[d] + y for d in range(1, far)] + [ahead[0] + 1 - y]:
        pl.semaphore_signal(
            barrier, inc=1, device_id={"ctx": where}, device_id_type=pl.DeviceIdType.MESH
        )
    pl.semaphore_wait(barrier, far)


def gather_kernel(n, q_ref, out_ref, own_sem, send_z, recv_z, send_y, recv_y):
    far, me, y, order, ahead, behind = places(n)
    pieces = q_ref.shape[0]
    local = pltpu.make_async_copy(q_ref, out_ref.at[me], own_sem)
    local.start()
    meet(far, y, ahead)
    sent = []
    for g in range(pieces):
        for d in order:
            sent.append(
                remote(q_ref.at[g], out_ref.at[me, g], send_z.at[d, g], recv_z.at[d, g], ahead[d] + y)
            )
            sent[-1].start()
        sent.append(
            remote(q_ref.at[g], out_ref.at[me, g], send_y.at[0, g], recv_y.at[0, g], ahead[0] + 1 - y)
        )
        sent[-1].start()
    for g in range(pieces):
        for d in order:
            got = out_ref.at[behind[d] + y, g]
            remote(got, got, send_z.at[d, g], recv_z.at[d, g], ahead[d] + y).wait_recv()
            sent.append(remote(got, got, send_y.at[d, g], recv_y.at[d, g], ahead[0] + 1 - y))
            sent[-1].start()
    for g in range(pieces):
        for d in range(far):
            got = out_ref.at[behind[d] + 1 - y, g]
            remote(got, got, send_y.at[d, g], recv_y.at[d, g], ahead[0] + 1 - y).wait_recv()
    for copy in sent:
        copy.wait_send()
    local.wait()


def weights_of(stats, kv, g):
    tops = stats[0][g : g + 1]
    for st in stats[1:]:
        tops = jnp.maximum(tops, st[g : g + 1])
    total = jnp.zeros_like(tops)
    lines = []
    for st in stats:
        w = jnp.exp(st[g : g + 1] - tops)
        total = total + st[kv + g : kv + g + 1] * w
        lines.append(st[2 * kv + g : 2 * kv + g + 1] * w)
    return tops, total, lines


def mixed(lines, partials):
    rows, hd = partials[0].shape
    size = min(rows, 128)
    table = jnp.concatenate(
        lines + [jnp.zeros_like(lines[0])] * (-len(lines) % 8), axis=0
    )
    outs = []
    for at in range(0, rows, size):
        cols = jnp.transpose(table[:, at : at + size])
        total = jnp.zeros((size, hd), F32)
        for i, part in enumerate(partials):
            total = total + cols[:, i : i + 1] * part[at : at + size].astype(jnp.int32).astype(F32)
        outs.append(total)
    return outs[0] if len(outs) == 1 else jnp.concatenate(outs, axis=0)


def reduce_kernel(
    n, kv, part_ref, st_ref, out_ref,
    pair_ref, pair_st, mix_ref, mix_st, line_ref, line_st,
    send_y, recv_y, send_z, recv_z,
):
    far, me, y, order, ahead, _ = places(n)
    rows = part_ref.shape[2]
    partner = ahead[0] + 1 - y
    meet(far, y, ahead)

    def to_pair(d):
        whose = ahead[d] + 1 - y
        return [
            remote(st_ref.at[whose], pair_st.at[d], send_y.at[d, kv], recv_y.at[d, kv], partner)
        ] + [
            remote(part_ref.at[whose, g], pair_ref.at[d, g], send_y.at[d, g], recv_y.at[d, g], partner)
            for g in range(kv)
        ]

    def to_line(d):
        return [
            remote(mix_st.at[d], line_st.at[d], send_z.at[d, kv], recv_z.at[d, kv], ahead[d] + y)
        ] + [
            remote(mix_ref.at[d, g], line_ref.at[d, g], send_z.at[d, g], recv_z.at[d, g], ahead[d] + y)
            for g in range(kv)
        ]

    pairs = {d: to_pair(d) for d in order + [0]}
    lines_out = {d: to_line(d) for d in order}
    for d in order + [0]:
        for copy in pairs[d]:
            copy.start()
    eye = eye_of(min(rows, 128))
    for d in order:
        pairs[d][0].wait_recv()
        whose = ahead[d] + y
        stats = [st_ref[whose], pair_st[d]]
        tops, totals, steps = [], [], []
        for g in range(kv):
            pairs[d][1 + g].wait_recv()
            top, total, lines = weights_of(stats, kv, g)
            coded, step = fixed(mixed(lines, [part_ref[whose, g], pair_ref[d, g]]))
            mix_ref[d, g] = coded
            tops.append(top)
            totals.append(total)
            steps.append(compact(step, eye))
            if g > 0:
                lines_out[d][g].start()
        pad = st_ref.shape[1] - 3 * kv
        mix_st[d] = jnp.concatenate(tops + totals + steps + [jnp.zeros((pad, rows), F32)], axis=0)
        lines_out[d][0].start()
        lines_out[d][kv].start()
    pairs[0][0].wait_recv()
    for d in order:
        lines_out[d][0].wait_recv()
    stats = [st_ref[me], pair_st[0]] + [line_st[d] for d in order]
    for g in range(kv):
        pairs[0][1 + g].wait_recv()
        for d in order:
            lines_out[d][1 + g].wait_recv()
        _, total, lines = weights_of(stats, kv, g)
        lines = [line / total for line in lines]
        partials = [part_ref[me, g], pair_ref[0, g]] + [line_ref[d, g] for d in order]
        out_ref[g] = mixed(lines, partials).astype(BF16)
    for d in order + [0]:
        for copy in pairs[d]:
            copy.wait_send()
    for d in order:
        for copy in lines_out[d]:
            copy.wait_send()


def per_device(queries, new_keys, new_values, history_keys, history_values, block_mask):
    _, own, heads, hd = queries.shape
    kv = new_keys.shape[2]
    group = heads // kv
    rows = own * group
    context = history_keys.shape[1]
    n = lax.axis_size("ctx")
    far = n // 2
    qblocks = block_mask.shape[1]
    chunks = BLK // own
    srows = -(-3 * kv // 8) * 8

    q = jnp.transpose(queries.reshape(own, kv, group, hd), (1, 0, 2, 3)).reshape(kv, rows, hd)
    k_new = new_keys.reshape(own, kv * hd)
    v_new = new_values.reshape(own, kv * hd)
    k_old = history_keys.reshape(context, kv * hd)
    v_old = history_values.reshape(context, kv * hd)
    vmem = pl.BlockSpec(memory_space=pltpu.VMEM)
    dma = pltpu.SemaphoreType.DMA

    q_all = pl.pallas_call(
        functools.partial(gather_kernel, n),
        in_specs=[vmem],
        out_specs=pl.BlockSpec(memory_space=pl.ANY),
        out_shape=jax.ShapeDtypeStruct((n, kv, rows, hd), BF16),
        scratch_shapes=[dma] + [dma((far, kv))] * 4,
        compiler_params=pltpu.CompilerParams(collective_id=0, has_side_effects=True),
        name="gather",
    )(q)

    part, stats = pl.pallas_call(
        functools.partial(hist_kernel, kv, own),
        grid_spec=pltpu.PrefetchScalarGridSpec(
            num_scalar_prefetch=1,
            grid=(qblocks, kv),
            in_specs=[
                pl.BlockSpec((chunks, 1, rows, hd), lambda b, g, m: (b, g, 0, 0)),
                pl.BlockSpec((context, hd), lambda b, g, m: (0, g)),
                pl.BlockSpec((context, hd), lambda b, g, m: (0, g)),
                pl.BlockSpec((own, hd), lambda b, g, m: (0, g)),
                pl.BlockSpec((own, hd), lambda b, g, m: (0, g)),
            ],
            out_specs=[
                pl.BlockSpec((chunks, 1, rows, hd), lambda b, g, m: (b, g, 0, 0)),
                pl.BlockSpec((chunks, srows, rows), lambda b, g, m: (b, 0, 0)),
            ],
            scratch_shapes=[
                pltpu.VMEM((chunks, rows, 2 * hd), F32),
                pltpu.VMEM((chunks, rows, hd), F32),
            ],
        ),
        out_shape=[
            jax.ShapeDtypeStruct((n, kv, rows, hd), jnp.int16),
            jax.ShapeDtypeStruct((n, srows, rows), F32),
        ],
        name="hist",
    )(block_mask[0], q_all, k_old, v_old, k_new, v_new)

    slots = [
        pltpu.VMEM((far, kv, rows, hd), jnp.int16),
        pltpu.VMEM((far, srows, rows), F32),
    ]
    out = pl.pallas_call(
        functools.partial(reduce_kernel, n, kv),
        in_specs=[vmem, vmem],
        out_specs=vmem,
        out_shape=jax.ShapeDtypeStruct((kv, rows, hd), BF16),
        scratch_shapes=slots * 3 + [dma((far, kv + 1))] * 4,
        compiler_params=pltpu.CompilerParams(collective_id=1, has_side_effects=True),
        name="reduce",
    )(part, stats)
    out = jnp.transpose(out.reshape(kv, own, group, hd), (1, 0, 2, 3))
    return out.reshape(1, own, heads, hd)


def solution(mesh):
    spec = P("groups", "ctx", "head", None)
    return jax.shard_map(
        per_device,
        mesh=mesh,
        in_specs=(spec,) * 5 + (P("groups", None, "ctx"),),
        out_specs=spec,
        check_vma=False,
    )
```

```python
import functools
import math

import jax
import jax.numpy as jnp
from jax import lax
from jax.experimental import pallas as pl
from jax.experimental.pallas import tpu as pltpu
from jax.sharding import PartitionSpec as P

BLK = 128
NEG = -1e30
TINY = 1e-30
TOP = 32767.0
F32 = jnp.float32
BF16 = jnp.bfloat16


def scores_of(q, k):
    return lax.dot_general(q, k, (((1,), (1,)), ((), ())), preferred_element_type=F32)


def weighted(p, v):
    hi = p.astype(BF16)
    lo = (p - hi.astype(F32)).astype(BF16)
    wide = jnp.concatenate([v, jnp.ones_like(v)], axis=1)
    return jnp.dot(hi, wide, preferred_element_type=F32) + jnp.dot(
        lo, wide, preferred_element_type=F32
    )


def compact(x, eye):
    rows = x.shape[0]
    size = eye.shape[0]
    parts = []
    for at in range(0, rows, size):
        piece = jnp.where(eye, x[at : at + size], 0.0)
        parts.append(jnp.sum(piece, axis=0, keepdims=True)[:, :size])
    return parts[0] if len(parts) == 1 else jnp.concatenate(parts, axis=1)


def eye_of(size):
    return lax.broadcasted_iota(jnp.int32, (size, 128), 0) == lax.broadcasted_iota(
        jnp.int32, (size, 128), 1
    )


def spread(p, v):
    hi = p.astype(BF16)
    lo = (p - hi.astype(F32)).astype(BF16)
    wide = jnp.concatenate([v, jnp.ones_like(v)], axis=1)
    return jnp.dot(
        jnp.concatenate([hi, lo], axis=1),
        jnp.concatenate([wide, wide], axis=0),
        preferred_element_type=F32,
    )


def fold(s, v, acc_ref, m_ref, c):
    old = m_ref[c]
    half = s.shape[1] // 2
    new = jnp.maximum(old, jnp.max(jnp.maximum(s[:, :half], s[:, half:]), axis=1, keepdims=True))
    alpha = jnp.exp(old - new)
    p = jnp.exp(s - jnp.concatenate([new, new], axis=1))
    m_ref[c] = new
    acc_ref[c] = acc_ref[c] * jnp.concatenate([alpha, alpha], axis=1) + spread(p, v)


def fixed(num):
    big = jnp.maximum(jnp.max(jnp.abs(num), axis=1, keepdims=True), TINY)
    coded = jnp.floor(num * (TOP / big) + 0.5).astype(jnp.int32).astype(jnp.int16)
    return coded, jnp.broadcast_to(big * (1.0 / TOP), num.shape)


def hist_kernel(kv, own, mask_ref, q_ref, k_ref, v_ref, kn_ref, vn_ref, o_ref, st_ref, acc_ref, m_ref, live_ref):
    chunks, _, rows, hd = q_ref.shape
    b, g = pl.program_id(0), pl.program_id(1)
    me = lax.axis_index("ctx")
    scale = 1.0 / math.sqrt(hd)
    blocks = k_ref.shape[0] // BLK
    count = jnp.int32(0)
    for j in range(blocks):
        live_ref[count] = j
        count = count + jnp.where(mask_ref[b, j] > 0, 1, 0)

    def taken(ref, i):
        j = jnp.where(i < count, live_ref[jnp.minimum(i, blocks)], 0)
        return ref[pl.ds(pl.multiple_of(j * BLK, BLK), BLK), :]

    blank = jnp.zeros((BLK - own, hd), BF16)
    k = jnp.concatenate([kn_ref[...], blank, taken(k_ref, 0)], axis=0)
    v = jnp.concatenate([vn_ref[...], blank, taken(v_ref, 0)], axis=0)
    col = lax.broadcasted_iota(jnp.int32, (rows, 2 * BLK), 1)
    query = lax.broadcasted_iota(jnp.int32, (rows, 2 * BLK), 0) // (rows // own)
    reach = jnp.where(count > 0, 2 * BLK, BLK)
    for c in range(chunks):
        last = jnp.minimum(query + ((b * chunks + c) - me) * own, own - 1)
        seen = (col <= last) | ((col >= BLK) & (col < reach))
        s = jnp.where(seen, scores_of(q_ref[c, 0], k) * scale, NEG)
        top = jnp.max(jnp.maximum(s[:, :BLK], s[:, BLK:]), axis=1, keepdims=True)
        m_ref[c] = jnp.broadcast_to(top, (rows, hd))
        acc_ref[c] = spread(jnp.where(seen, jnp.exp(s - top), 0.0), v)

    @pl.loop(0, count // 2)
    def _(t):
        i = 1 + 2 * t
        k = jnp.concatenate([taken(k_ref, i), taken(k_ref, i + 1)], axis=0)
        v = jnp.concatenate([taken(v_ref, i), taken(v_ref, i + 1)], axis=0)
        reach = jnp.where(i + 1 < count, 2 * BLK, BLK)
        col = lax.broadcasted_iota(jnp.int32, (rows, 2 * BLK), 1)
        for c in range(chunks):
            s = jnp.where(col < reach, scores_of(q_ref[c, 0], k) * scale, NEG)
            fold(s, v, acc_ref, m_ref, c)

    eye = eye_of(min(rows, 128))
    for c in range(chunks):
        acc = acc_ref[c]
        coded, step = fixed(acc[:, :hd])
        o_ref[c, 0] = coded
        st_ref[c, pl.ds(g, 1)] = compact(m_ref[c], eye)
        st_ref[c, pl.ds(kv + g, 1)] = compact(acc[:, hd:], eye)
        st_ref[c, pl.ds(2 * kv + g, 1)] = compact(step, eye)


def remote(src, dst, send, recv, where):
    return pltpu.make_async_remote_copy(
        src_ref=src,
        dst_ref=dst,
        send_sem=send,
        recv_sem=recv,
        device_id={"ctx": where},
        device_id_type=pl.DeviceIdType.MESH,
    )


def places(n):
    far = n // 2
    me = lax.axis_index("ctx")
    z, y = me // 2, me % 2
    order = sorted(range(1, far), key=lambda d: abs(2 * d - far))
    ahead = [((z + d) % far) * 2 for d in range(far)]
    behind = [((z + far - d) % far) * 2 for d in range(far)]
    return far, me, y, order, ahead, behind


def meet(far, y, ahead):
    barrier = pltpu.get_barrier_semaphore()
    for where in [ahead[d] + y for d in range(1, far)] + [ahead[0] + 1 - y]:
        pl.semaphore_signal(
            barrier, inc=1, device_id={"ctx": where}, device_id_type=pl.DeviceIdType.MESH
        )
    pl.semaphore_wait(barrier, far)


def gather_kernel(n, q_ref, out_ref, own_sem, send_z, recv_z, send_y, recv_y):
    far, me, y, order, ahead, behind = places(n)
    pieces = q_ref.shape[0]
    local = pltpu.make_async_copy(q_ref, out_ref.at[me], own_sem)
    local.start()
    meet(far, y, ahead)
    sent = []
    for g in range(pieces):
        for d in order:
            sent.append(
                remote(q_ref.at[g], out_ref.at[me, g], send_z.at[d, g], recv_z.at[d, g], ahead[d] + y)
            )
            sent[-1].start()
        sent.append(
            remote(q_ref.at[g], out_ref.at[me, g], send_y.at[0, g], recv_y.at[0, g], ahead[0] + 1 - y)
        )
        sent[-1].start()
    for g in range(pieces):
        for d in order:
            got = out_ref.at[behind[d] + y, g]
            remote(got, got, send_z.at[d, g], recv_z.at[d, g], ahead[d] + y).wait_recv()
            sent.append(remote(got, got, send_y.at[d, g], recv_y.at[d, g], ahead[0] + 1 - y))
            sent[-1].start()
    for g in range(pieces):
        for d in range(far):
            got = out_ref.at[behind[d] + 1 - y, g]
            remote(got, got, send_y.at[d, g], recv_y.at[d, g], ahead[0] + 1 - y).wait_recv()
    for copy in sent:
        copy.wait_send()
    local.wait()


def weights_of(stats, kv, g):
    tops = stats[0][g : g + 1]
    for st in stats[1:]:
        tops = jnp.maximum(tops, st[g : g + 1])
    total = jnp.zeros_like(tops)
    lines = []
    for st in stats:
        w = jnp.exp(st[g : g + 1] - tops)
        total = total + st[kv + g : kv + g + 1] * w
        lines.append(st[2 * kv + g : 2 * kv + g + 1] * w)
    return tops, total, lines


def mixed(lines, partials):
    rows, hd = partials[0].shape
    size = min(rows, 128)
    table = jnp.concatenate(
        lines + [jnp.zeros_like(lines[0])] * (-len(lines) % 8), axis=0
    )
    outs = []
    for at in range(0, rows, size):
        cols = jnp.transpose(table[:, at : at + size])
        total = jnp.zeros((size, hd), F32)
        for i, part in enumerate(partials):
            total = total + cols[:, i : i + 1] * part[at : at + size].astype(jnp.int32).astype(F32)
        outs.append(total)
    return outs[0] if len(outs) == 1 else jnp.concatenate(outs, axis=0)


def reduce_kernel(
    n, kv, part_ref, st_ref, out_ref,
    pair_ref, pair_st, mix_ref, mix_st, line_ref, line_st,
    send_y, recv_y, send_z, recv_z,
):
    far, me, y, order, ahead, _ = places(n)
    rows = part_ref.shape[2]
    partner = ahead[0] + 1 - y
    meet(far, y, ahead)

    def to_pair(d):
        whose = ahead[d] + 1 - y
        return [
            remote(st_ref.at[whose], pair_st.at[d], send_y.at[d, kv], recv_y.at[d, kv], partner)
        ] + [
            remote(part_ref.at[whose, g], pair_ref.at[d, g], send_y.at[d, g], recv_y.at[d, g], partner)
            for g in range(kv)
        ]

    def to_line(d):
        return [
            remote(mix_st.at[d], line_st.at[d], send_z.at[d, kv], recv_z.at[d, kv], ahead[d] + y)
        ] + [
            remote(mix_ref.at[d, g], line_ref.at[d, g], send_z.at[d, g], recv_z.at[d, g], ahead[d] + y)
            for g in range(kv)
        ]

    pairs = {d: to_pair(d) for d in order + [0]}
    lines_out = {d: to_line(d) for d in order}
    for d in order + [0]:
        for copy in pairs[d]:
            copy.start()
    eye = eye_of(min(rows, 128))
    for d in order:
        pairs[d][0].wait_recv()
        whose = ahead[d] + y
        stats = [st_ref[whose], pair_st[d]]
        tops, totals, steps = [], [], []
        for g in range(kv):
            pairs[d][1 + g].wait_recv()
            top, total, lines = weights_of(stats, kv, g)
            coded, step = fixed(mixed(lines, [part_ref[whose, g], pair_ref[d, g]]))
            mix_ref[d, g] = coded
            tops.append(top)
            totals.append(total)
            steps.append(compact(step, eye))
            if g > 0:
                lines_out[d][g].start()
        pad = st_ref.shape[1] - 3 * kv
        mix_st[d] = jnp.concatenate(tops + totals + steps + [jnp.zeros((pad, rows), F32)], axis=0)
        lines_out[d][0].start()
        lines_out[d][kv].start()
    pairs[0][0].wait_recv()
    for d in order:
        lines_out[d][0].wait_recv()
    stats = [st_ref[me], pair_st[0]] + [line_st[d] for d in order]
    for g in range(kv):
        pairs[0][1 + g].wait_recv()
        for d in order:
            lines_out[d][1 + g].wait_recv()
        _, total, lines = weights_of(stats, kv, g)
        lines = [line / total for line in lines]
        partials = [part_ref[me, g], pair_ref[0, g]] + [line_ref[d, g] for d in order]
        out_ref[g] = mixed(lines, partials).astype(BF16)
    for d in order + [0]:
        for copy in pairs[d]:
            copy.wait_send()
    for d in order:
        for copy in lines_out[d]:
            copy.wait_send()


def per_device(queries, new_keys, new_values, history_keys, history_values, block_mask):
    _, own, heads, hd = queries.shape
    kv = new_keys.shape[2]
    group = heads // kv
    rows = own * group
    context = history_keys.shape[1]
    n = lax.axis_size("ctx")
    far = n // 2
    qblocks = block_mask.shape[1]
    chunks = BLK // own
    srows = -(-3 * kv // 8) * 8

    q = jnp.transpose(queries.reshape(own, kv, group, hd), (1, 0, 2, 3)).reshape(kv, rows, hd)
    k_new = new_keys.reshape(own, kv * hd)
    v_new = new_values.reshape(own, kv * hd)
    k_old = history_keys.reshape(context, kv * hd)
    v_old = history_values.reshape(context, kv * hd)
    vmem = pl.BlockSpec(memory_space=pltpu.VMEM)
    dma = pltpu.SemaphoreType.DMA

    q_all = pl.pallas_call(
        functools.partial(gather_kernel, n),
        in_specs=[vmem],
        out_specs=pl.BlockSpec(memory_space=pl.ANY),
        out_shape=jax.ShapeDtypeStruct((n, kv, rows, hd), BF16),
        scratch_shapes=[dma] + [dma((far, kv))] * 4,
        compiler_params=pltpu.CompilerParams(collective_id=0, has_side_effects=True),
        name="gather",
    )(q)

    part, stats = pl.pallas_call(
        functools.partial(hist_kernel, kv, own),
        grid_spec=pltpu.PrefetchScalarGridSpec(
            num_scalar_prefetch=1,
            grid=(qblocks, kv),
            in_specs=[
                pl.BlockSpec((chunks, 1, rows, hd), lambda b, g, m: (b, g, 0, 0)),
                pl.BlockSpec((context, hd), lambda b, g, m: (0, g)),
                pl.BlockSpec((context, hd), lambda b, g, m: (0, g)),
                pl.BlockSpec((own, hd), lambda b, g, m: (0, g)),
                pl.BlockSpec((own, hd), lambda b, g, m: (0, g)),
            ],
            out_specs=[
                pl.BlockSpec((chunks, 1, rows, hd), lambda b, g, m: (b, g, 0, 0)),
                pl.BlockSpec((chunks, srows, rows), lambda b, g, m: (b, 0, 0)),
            ],
            scratch_shapes=[
                pltpu.VMEM((chunks, rows, 2 * hd), F32),
                pltpu.VMEM((chunks, rows, hd), F32),
                pltpu.SMEM((context // BLK + 1,), jnp.int32),
            ],
        ),
        out_shape=[
            jax.ShapeDtypeStruct((n, kv, rows, hd), jnp.int16),
            jax.ShapeDtypeStruct((n, srows, rows), F32),
        ],
        name="hist",
    )(block_mask[0], q_all, k_old, v_old, k_new, v_new)

    slots = [
        pltpu.VMEM((far, kv, rows, hd), jnp.int16),
        pltpu.VMEM((far, srows, rows), F32),
    ]
    out = pl.pallas_call(
        functools.partial(reduce_kernel, n, kv),
        in_specs=[vmem, vmem],
        out_specs=vmem,
        out_shape=jax.ShapeDtypeStruct((kv, rows, hd), BF16),
        scratch_shapes=slots * 3 + [dma((far, kv + 1))] * 4,
        compiler_params=pltpu.CompilerParams(collective_id=1, has_side_effects=True),
        name="reduce",
    )(part, stats)
    out = jnp.transpose(out.reshape(kv, own, group, hd), (1, 0, 2, 3))
    return out.reshape(1, own, heads, hd)


def solution(mesh):
    spec = P("groups", "ctx", "head", None)
    return jax.shard_map(
        per_device,
        mesh=mesh,
        in_specs=(spec,) * 5 + (P("groups", None, "ctx"),),
        out_specs=spec,
        check_vma=False,
    )
```

```python
import functools
import math

import jax
import jax.numpy as jnp
from jax import lax
from jax.experimental import pallas as pl
from jax.experimental.pallas import tpu as pltpu
from jax.sharding import PartitionSpec as P

BLK = 128
NEG = -1e30
TINY = 1e-30
TOP = 32767.0
F32 = jnp.float32
BF16 = jnp.bfloat16


def scores_of(q, k):
    return lax.dot_general(q, k, (((1,), (1,)), ((), ())), preferred_element_type=F32)


def compact(x, eye):
    rows = x.shape[0]
    size = eye.shape[0]
    parts = []
    for at in range(0, rows, size):
        piece = jnp.where(eye, x[at : at + size], 0.0)
        parts.append(jnp.sum(piece, axis=0, keepdims=True)[:, :size])
    return parts[0] if len(parts) == 1 else jnp.concatenate(parts, axis=1)


def eye_of(size):
    return lax.broadcasted_iota(jnp.int32, (size, 128), 0) == lax.broadcasted_iota(
        jnp.int32, (size, 128), 1
    )


def spread(p, v):
    hi = p.astype(BF16)
    lo = (p - hi.astype(F32)).astype(BF16)
    wide = jnp.concatenate([v, jnp.ones_like(v)], axis=1)
    return jnp.dot(
        jnp.concatenate([hi, lo], axis=1),
        jnp.concatenate([wide, wide], axis=0),
        preferred_element_type=F32,
    )


def fixed(num):
    big = jnp.maximum(jnp.max(jnp.abs(num), axis=1, keepdims=True), TINY)
    coded = jnp.floor(num * (TOP / big) + 0.5).astype(jnp.int32).astype(jnp.int16)
    return coded, jnp.broadcast_to(big * (1.0 / TOP), num.shape)


def remote(src, dst, send, recv, where):
    return pltpu.make_async_remote_copy(
        src_ref=src,
        dst_ref=dst,
        send_sem=send,
        recv_sem=recv,
        device_id={"ctx": where},
        device_id_type=pl.DeviceIdType.MESH,
    )


def places(n):
    far = n // 2
    me = lax.axis_index("ctx")
    z, y = me // 2, me % 2
    order = sorted(range(1, far), key=lambda d: abs(2 * d - far))
    ahead = [((z + d) % far) * 2 for d in range(far)]
    behind = [((z + far - d) % far) * 2 for d in range(far)]
    return far, me, y, order, ahead, behind


def meet(far, y, ahead):
    barrier = pltpu.get_barrier_semaphore()
    for where in [ahead[d] + y for d in range(1, far)] + [ahead[0] + 1 - y]:
        pl.semaphore_signal(
            barrier, inc=1, device_id={"ctx": where}, device_id_type=pl.DeviceIdType.MESH
        )
    pl.semaphore_wait(barrier, far)


def weights_of(stats):
    tops = stats[0][0:1]
    for st in stats[1:]:
        tops = jnp.maximum(tops, st[0:1])
    total = jnp.zeros_like(tops)
    lines = []
    for st in stats:
        w = jnp.exp2(st[0:1] - tops)
        total = total + st[1:2] * w
        lines.append(st[2:3] * w)
    return tops, total, lines


def fused_kernel(
    n, kv, own, mask_ref, q_ref, k_ref, v_ref, kn_ref, vn_ref, out_ref,
    all_ref, s_ref, part_ref, part_st, pair_ref, pair_st, mix_ref, mix_st, line_ref, line_st,
    send_z, recv_z, send_y, recv_y, send_p, recv_p, send_l, recv_l,
):
    far, me, y, order, ahead, behind = places(n)
    rows, hd = q_ref.shape[1:]
    partner = ahead[0] + 1 - y
    z = me // 2
    chunks = BLK // own
    pairs = k_ref.shape[0] // (2 * BLK)
    factor = math.log2(math.e) / math.sqrt(hd)
    eye = eye_of(min(rows, 128))

    meet(far, y, ahead)
    waits = []
    for g in range(kv):
        for d in order:
            waits.append(
                remote(q_ref.at[g], all_ref.at[me, g], send_z.at[d, g], recv_z.at[d, g], ahead[d] + y)
            )
            waits[-1].start()
        waits.append(
            remote(q_ref.at[g], all_ref.at[me, g], send_y.at[0, g], recv_y.at[0, g], partner)
        )
        waits[-1].start()
    all_ref[me] = q_ref[...]

    def relay(g):
        for d in order:
            got = all_ref.at[behind[d] + y, g]
            remote(got, got, send_z.at[d, g], recv_z.at[d, g], ahead[d] + y).wait_recv()
            waits.append(remote(got, got, send_y.at[d, g], recv_y.at[d, g], partner))
            waits[-1].start()

    def arrive(g):
        for d in range(far):
            got = all_ref.at[behind[d] + 1 - y, g]
            remote(got, got, send_y.at[d, g], recv_y.at[d, g], partner).wait_recv()

    def attend(idx, g):
        b = idx // chunks
        q = all_ref[idx, g]
        lanes = slice(g * hd, (g + 1) * hd)
        blank = jnp.zeros((BLK - own, hd), BF16)
        col = lax.broadcasted_iota(jnp.int32, (rows, BLK), 1)
        query = lax.broadcasted_iota(jnp.int32, (rows, BLK), 0) // (rows // own)
        seen = col <= jnp.minimum(query + (idx - me) * own, own - 1)
        s = scores_of(q, jnp.concatenate([kn_ref[:, lanes], blank], axis=0))
        fresh = jnp.where(seen, s * factor, NEG)
        top = fresh
        for t in range(pairs):
            s = scores_of(q, k_ref[t * 2 * BLK : (t + 1) * 2 * BLK, lanes]) * factor
            for half in range(2):
                part = s[:, half * BLK : (half + 1) * BLK]
                part = jnp.where(mask_ref[b, 2 * t + half] > 0, part, NEG)
                s_ref[2 * t + half] = part
                top = jnp.maximum(top, part)
        peak = jnp.maximum(jnp.max(top, axis=1, keepdims=True), 0.5 * NEG)
        acc = spread(
            jnp.exp2(fresh - peak), jnp.concatenate([vn_ref[:, lanes], blank], axis=0)
        )
        for t in range(pairs):
            p = jnp.concatenate(
                [jnp.exp2(s_ref[2 * t] - peak), jnp.exp2(s_ref[2 * t + 1] - peak)], axis=1
            )
            acc = acc + spread(p, v_ref[t * 2 * BLK : (t + 1) * 2 * BLK, lanes])
        coded, step = fixed(acc[:, :hd])
        part_ref[idx, g] = coded
        part_st[idx, g] = jnp.concatenate(
            [
                compact(jnp.broadcast_to(peak, (rows, hd)), eye),
                compact(acc[:, hd:], eye),
                compact(step, eye),
                jnp.zeros((5, rows), F32),
            ],
            axis=0,
        )

    def to_pair(d, g):
        whose = ahead[d] + 1 - y
        return (
            remote(part_st.at[whose, g], pair_st.at[d, g], send_p.at[d, g, 0], recv_p.at[d, g, 0], partner),
            remote(part_ref.at[whose, g], pair_ref.at[d, g], send_p.at[d, g, 1], recv_p.at[d, g, 1], partner),
        )

    def to_line(d, g):
        whose = ahead[d] + y
        return (
            remote(mix_st.at[d, g], line_st.at[d, g], send_l.at[d, g, 0], recv_l.at[d, g, 0], whose),
            remote(mix_ref.at[d, g], line_ref.at[d, g], send_l.at[d, g, 1], recv_l.at[d, g, 1], whose),
        )

    def merge(g):
        for d in order:
            for copy in to_pair(d, g):
                copy.wait_recv()
            whose = ahead[d] + y
            top, total, lines = weights_of([part_st[whose, g], pair_st[d, g]])
            coded, step = fixed(mixed(lines, [part_ref[whose, g], pair_ref[d, g]]))
            mix_ref[d, g] = coded
            mix_st[d, g] = jnp.concatenate(
                [top, total, compact(step, eye), jnp.zeros((5, rows), F32)], axis=0
            )
        for d in order:
            for copy in to_line(d, g):
                copy.start()
                waits.append(copy)

    def finish(g):
        for copy in to_pair(0, g):
            copy.wait_recv()
        for d in order:
            for copy in to_line(d, g):
                copy.wait_recv()
        _, total, lines = weights_of(
            [part_st[me, g], pair_st[0, g]] + [line_st[d, g] for d in order]
        )
        lines = [line / total for line in lines]
        partials = [part_ref[me, g], pair_ref[0, g]] + [line_ref[d, g] for d in order]
        out_ref[g] = mixed(lines, partials).astype(BF16)

    relay(0)
    for g in range(kv):
        arrive(g)

        @pl.loop(0, far)
        def _(t):
            attend(lax.rem(z + t, far) * 2 + 1 - y, g)

        for d in order + [0]:
            for copy in to_pair(d, g):
                copy.start()
                waits.append(copy)
        if g + 1 < kv:
            relay(g + 1)

        @pl.loop(0, far)
        def _(t):
            attend(lax.rem(z + t, far) * 2 + y, g)

        if g > 0:
            merge(g - 1)
        if g > 1:
            finish(g - 2)
    merge(kv - 1)
    for g in range(max(kv - 2, 0), kv):
        finish(g)
    for copy in waits:
        copy.wait_send()


def per_device(queries, new_keys, new_values, history_keys, history_values, block_mask):
    _, own, heads, hd = queries.shape
    kv = new_keys.shape[2]
    group = heads // kv
    rows = own * group
    context = history_keys.shape[1]
    n = lax.axis_size("ctx")
    far = n // 2

    q = jnp.transpose(queries.reshape(own, kv, group, hd), (1, 0, 2, 3)).reshape(kv, rows, hd)
    vmem = pl.BlockSpec(memory_space=pltpu.VMEM)
    dma = pltpu.SemaphoreType.DMA
    slots = [
        pltpu.VMEM((far, kv, rows, hd), jnp.int16),
        pltpu.VMEM((far, kv, 8, rows), F32),
    ]
    out = pl.pallas_call(
        functools.partial(fused_kernel, n, kv, own),
        in_specs=[pl.BlockSpec(memory_space=pltpu.SMEM)] + [vmem] * 5,
        out_specs=vmem,
        out_shape=jax.ShapeDtypeStruct((kv, rows, hd), BF16),
        scratch_shapes=[
            pltpu.VMEM((n, kv, rows, hd), BF16),
            pltpu.VMEM((context // BLK, rows, BLK), F32),
            pltpu.VMEM((n, kv, rows, hd), jnp.int16),
            pltpu.VMEM((n, kv, 8, rows), F32),
        ]
        + slots * 3
        + [dma((far, kv))] * 4
        + [dma((far, kv, 2))] * 4,
        compiler_params=pltpu.CompilerParams(collective_id=0, has_side_effects=True),
        name="fused",
    )(
        block_mask[0],
        q,
        history_keys.reshape(context, kv * hd),
        history_values.reshape(context, kv * hd),
        new_keys.reshape(own, kv * hd),
        new_values.reshape(own, kv * hd),
    )
    out = jnp.transpose(out.reshape(kv, own, group, hd), (1, 0, 2, 3))
    return out.reshape(1, own, heads, hd)


def mixed(lines, partials):
    rows, hd = partials[0].shape
    size = min(rows, 128)
    table = jnp.concatenate(
        lines + [jnp.zeros_like(lines[0])] * (-len(lines) % 8), axis=0
    )
    outs = []
    for at in range(0, rows, size):
        cols = jnp.transpose(table[:, at : at + size])
        total = jnp.zeros((size, hd), F32)
        for i, part in enumerate(partials):
            total = total + cols[:, i : i + 1] * part[at : at + size].astype(jnp.int32).astype(F32)
        outs.append(total)
    return outs[0] if len(outs) == 1 else jnp.concatenate(outs, axis=0)


def solution(mesh):
    spec = P("groups", "ctx", "head", None)
    return jax.shard_map(
        per_device,
        mesh=mesh,
        in_specs=(spec,) * 5 + (P("groups", None, "ctx"),),
        out_specs=spec,
        check_vma=False,
    )
```

```python
import functools
import math

import jax
import jax.numpy as jnp
from jax import lax
from jax.experimental import pallas as pl
from jax.experimental.pallas import tpu as pltpu
from jax.sharding import PartitionSpec as P

BLK = 128
NEG = -1e30
TINY = 1e-30
TOP = 32767.0
F32 = jnp.float32
BF16 = jnp.bfloat16


def scores_of(q, k):
    return lax.dot_general(q, k, (((1,), (1,)), ((), ())), preferred_element_type=F32)


def compact(x, eye):
    rows = x.shape[0]
    size = eye.shape[0]
    parts = []
    for at in range(0, rows, size):
        piece = jnp.where(eye, x[at : at + size], 0.0)
        parts.append(jnp.sum(piece, axis=0, keepdims=True)[:, :size])
    return parts[0] if len(parts) == 1 else jnp.concatenate(parts, axis=1)


def eye_of(size):
    return lax.broadcasted_iota(jnp.int32, (size, 128), 0) == lax.broadcasted_iota(
        jnp.int32, (size, 128), 1
    )


def fixed(num):
    big = jnp.maximum(jnp.max(jnp.abs(num), axis=1, keepdims=True), TINY)
    coded = jnp.floor(num * (TOP / big) + 0.5).astype(jnp.int32).astype(jnp.int16)
    return coded, jnp.broadcast_to(big * (1.0 / TOP), num.shape)


def remote(src, dst, send, recv, where):
    return pltpu.make_async_remote_copy(
        src_ref=src,
        dst_ref=dst,
        send_sem=send,
        recv_sem=recv,
        device_id={"ctx": where},
        device_id_type=pl.DeviceIdType.MESH,
    )


def places(n):
    far = n // 2
    me = lax.axis_index("ctx")
    z, y = me // 2, me % 2
    order = sorted(range(1, far), key=lambda d: abs(2 * d - far))
    ahead = [((z + d) % far) * 2 for d in range(far)]
    behind = [((z + far - d) % far) * 2 for d in range(far)]
    return far, me, y, order, ahead, behind


def meet(far, y, ahead):
    barrier = pltpu.get_barrier_semaphore()
    for where in [ahead[d] + y for d in range(1, far)] + [ahead[0] + 1 - y]:
        pl.semaphore_signal(
            barrier, inc=1, device_id={"ctx": where}, device_id_type=pl.DeviceIdType.MESH
        )
    pl.semaphore_wait(barrier, far)


def weights_of(stats):
    tops = stats[0][0:1]
    for st in stats[1:]:
        tops = jnp.maximum(tops, st[0:1])
    total = jnp.zeros_like(tops)
    lines = []
    for st in stats:
        w = jnp.exp2(st[0:1] - tops)
        total = total + st[1:2] * w
        lines.append(st[2:3] * w)
    return tops, total, lines


def fused_kernel(
    n, kv, own, mask_ref, q_ref, k_ref, v_ref, kn_ref, vn_ref, out_ref,
    all_ref, s_ref, p_ref, wide_ref, part_ref, part_st, pair_ref, pair_st, mix_ref, mix_st, line_ref, line_st,
    send_z, recv_z, send_y, recv_y, send_p, recv_p, send_l, recv_l,
):
    far, me, y, order, ahead, behind = places(n)
    rows, hd = q_ref.shape[1:]
    partner = ahead[0] + 1 - y
    z = me // 2
    chunks = BLK // own
    pairs = k_ref.shape[0] // (2 * BLK)
    factor = math.log2(math.e) / math.sqrt(hd)
    eye = eye_of(min(rows, 128))

    meet(far, y, ahead)
    waits = []
    for g in range(kv):
        for d in order:
            waits.append(
                remote(q_ref.at[g], all_ref.at[me, g], send_z.at[d, g], recv_z.at[d, g], ahead[d] + y)
            )
            waits[-1].start()
        waits.append(
            remote(q_ref.at[g], all_ref.at[me, g], send_y.at[0, g], recv_y.at[0, g], partner)
        )
        waits[-1].start()
    all_ref[me] = q_ref[...]

    def relay(g):
        for d in order:
            got = all_ref.at[behind[d] + y, g]
            remote(got, got, send_z.at[d, g], recv_z.at[d, g], ahead[d] + y).wait_recv()
            waits.append(remote(got, got, send_y.at[d, g], recv_y.at[d, g], partner))
            waits[-1].start()

    def arrive(g):
        for d in range(far):
            got = all_ref.at[behind[d] + 1 - y, g]
            remote(got, got, send_y.at[d, g], recv_y.at[d, g], partner).wait_recv()

    def widen(g):
        lanes = slice(g * hd, (g + 1) * hd)
        blank = jnp.zeros((BLK - own, hd), BF16)
        ones = jnp.ones((2 * BLK, hd), BF16)
        fresh = jnp.concatenate([vn_ref[:, lanes], blank], axis=0)
        wide_ref[: 2 * BLK, :hd] = jnp.concatenate([fresh, fresh], axis=0)
        wide_ref[: 2 * BLK, hd:] = ones
        for t in range(pairs):
            v = v_ref[t * 2 * BLK : (t + 1) * 2 * BLK, lanes]
            for copy in range(2):
                at = 2 * BLK * (1 + 2 * t + copy)
                wide_ref[at : at + 2 * BLK, :hd] = v
                wide_ref[at : at + 2 * BLK, hd:] = ones

    def split(at, p):
        cols = p.shape[1]
        hi = p.astype(BF16)
        p_ref[:, at : at + cols] = hi
        p_ref[:, at + cols : at + 2 * cols] = (p - hi.astype(F32)).astype(BF16)

    def attend(both, g):
        q = jnp.concatenate([all_ref[idx, g] for idx in both], axis=0)
        lanes = slice(g * hd, (g + 1) * hd)
        blank = jnp.zeros((BLK - own, hd), BF16)
        col = lax.broadcasted_iota(jnp.int32, (rows, BLK), 1)
        query = lax.broadcasted_iota(jnp.int32, (rows, BLK), 0) // (rows // own)
        s = scores_of(q, jnp.concatenate([kn_ref[:, lanes], blank], axis=0)) * factor
        fresh = jnp.concatenate(
            [
                jnp.where(
                    col <= jnp.minimum(query + (idx - me) * own, own - 1),
                    s[i * rows : (i + 1) * rows],
                    NEG,
                )
                for i, idx in enumerate(both)
            ],
            axis=0,
        )
        top = fresh
        for t in range(pairs):
            s = scores_of(q, k_ref[t * 2 * BLK : (t + 1) * 2 * BLK, lanes]) * factor
            for half in range(2):
                part = s[:, half * BLK : (half + 1) * BLK]
                part = jnp.concatenate(
                    [
                        jnp.where(
                            mask_ref[idx // chunks, 2 * t + half] > 0,
                            part[i * rows : (i + 1) * rows],
                            NEG,
                        )
                        for i, idx in enumerate(both)
                    ],
                    axis=0,
                )
                s_ref[2 * t + half] = part
                top = jnp.maximum(top, part)
        peak = jnp.maximum(jnp.max(top, axis=1, keepdims=True), 0.5 * NEG)
        split(0, jnp.exp2(fresh - peak))
        for t in range(pairs):
            p = jnp.concatenate(
                [jnp.exp2(s_ref[2 * t] - peak), jnp.exp2(s_ref[2 * t + 1] - peak)], axis=1
            )
            split(2 * BLK * (1 + 2 * t), p)
        acc = jnp.dot(p_ref[...], wide_ref[...], preferred_element_type=F32)
        coded, step = fixed(acc[:, :hd])
        peak = jnp.broadcast_to(peak, coded.shape)
        for i, idx in enumerate(both):
            at = slice(i * rows, (i + 1) * rows)
            part_ref[idx, g] = coded[at]
            part_st[idx, g] = jnp.concatenate(
                [
                    compact(peak[at], eye),
                    compact(acc[at, hd:], eye),
                    compact(step[at], eye),
                    jnp.zeros((5, rows), F32),
                ],
                axis=0,
            )

    def to_pair(d, g):
        whose = ahead[d] + 1 - y
        return (
            remote(part_st.at[whose, g], pair_st.at[d, g], send_p.at[d, g, 0], recv_p.at[d, g, 0], partner),
            remote(part_ref.at[whose, g], pair_ref.at[d, g], send_p.at[d, g, 1], recv_p.at[d, g, 1], partner),
        )

    def to_line(d, g):
        whose = ahead[d] + y
        return (
            remote(mix_st.at[d, g], line_st.at[d, g], send_l.at[d, g, 0], recv_l.at[d, g, 0], whose),
            remote(mix_ref.at[d, g], line_ref.at[d, g], send_l.at[d, g, 1], recv_l.at[d, g, 1], whose),
        )

    def merge(g):
        for d in order:
            for copy in to_pair(d, g):
                copy.wait_recv()
            whose = ahead[d] + y
            top, total, lines = weights_of([part_st[whose, g], pair_st[d, g]])
            coded, step = fixed(mixed(lines, [part_ref[whose, g], pair_ref[d, g]]))
            mix_ref[d, g] = coded
            mix_st[d, g] = jnp.concatenate(
                [top, total, compact(step, eye), jnp.zeros((5, rows), F32)], axis=0
            )
        for d in order:
            for copy in to_line(d, g):
                copy.start()
                waits.append(copy)

    def finish(g):
        for copy in to_pair(0, g):
            copy.wait_recv()
        for d in order:
            for copy in to_line(d, g):
                copy.wait_recv()
        _, total, lines = weights_of(
            [part_st[me, g], pair_st[0, g]] + [line_st[d, g] for d in order]
        )
        lines = [line / total for line in lines]
        partials = [part_ref[me, g], pair_ref[0, g]] + [line_ref[d, g] for d in order]
        out_ref[g] = mixed(lines, partials).astype(BF16)

    relay(0)
    for g in range(kv):
        widen(g)
        arrive(g)

        @pl.loop(0, far // 2)
        def _(t):
            attend([lax.rem(z + 2 * t + i, far) * 2 + 1 - y for i in range(2)], g)

        for d in order + [0]:
            for copy in to_pair(d, g):
                copy.start()
                waits.append(copy)
        if g + 1 < kv:
            relay(g + 1)

        @pl.loop(0, far // 2)
        def _(t):
            attend([lax.rem(z + 2 * t + i, far) * 2 + y for i in range(2)], g)

        if g > 0:
            merge(g - 1)
        if g > 1:
            finish(g - 2)
    merge(kv - 1)
    for g in range(max(kv - 2, 0), kv):
        finish(g)
    for copy in waits:
        copy.wait_send()


def per_device(queries, new_keys, new_values, history_keys, history_values, block_mask):
    _, own, heads, hd = queries.shape
    kv = new_keys.shape[2]
    group = heads // kv
    rows = own * group
    context = history_keys.shape[1]
    n = lax.axis_size("ctx")
    far = n // 2

    q = jnp.transpose(queries.reshape(own, kv, group, hd), (1, 0, 2, 3)).reshape(kv, rows, hd)
    vmem = pl.BlockSpec(memory_space=pltpu.VMEM)
    dma = pltpu.SemaphoreType.DMA
    slots = [
        pltpu.VMEM((far, kv, rows, hd), jnp.int16),
        pltpu.VMEM((far, kv, 8, rows), F32),
    ]
    out = pl.pallas_call(
        functools.partial(fused_kernel, n, kv, own),
        in_specs=[pl.BlockSpec(memory_space=pltpu.SMEM)] + [vmem] * 5,
        out_specs=vmem,
        out_shape=jax.ShapeDtypeStruct((kv, rows, hd), BF16),
        scratch_shapes=[
            pltpu.VMEM((n, kv, rows, hd), BF16),
            pltpu.VMEM((context // BLK, 2 * rows, BLK), F32),
            pltpu.VMEM((2 * rows, 2 * (context + BLK)), BF16),
            pltpu.VMEM((2 * (context + BLK), 2 * hd), BF16),
            pltpu.VMEM((n, kv, rows, hd), jnp.int16),
            pltpu.VMEM((n, kv, 8, rows), F32),
        ]
        + slots * 3
        + [dma((far, kv))] * 4
        + [dma((far, kv, 2))] * 4,
        compiler_params=pltpu.CompilerParams(collective_id=0, has_side_effects=True),
        name="fused",
    )(
        block_mask[0],
        q,
        history_keys.reshape(context, kv * hd),
        history_values.reshape(context, kv * hd),
        new_keys.reshape(own, kv * hd),
        new_values.reshape(own, kv * hd),
    )
    out = jnp.transpose(out.reshape(kv, own, group, hd), (1, 0, 2, 3))
    return out.reshape(1, own, heads, hd)


def mixed(lines, partials):
    rows, hd = partials[0].shape
    size = min(rows, 128)
    table = jnp.concatenate(
        lines + [jnp.zeros_like(lines[0])] * (-len(lines) % 8), axis=0
    )
    outs = []
    for at in range(0, rows, size):
        cols = jnp.transpose(table[:, at : at + size])
        total = jnp.zeros((size, hd), F32)
        for i, part in enumerate(partials):
            total = total + cols[:, i : i + 1] * part[at : at + size].astype(jnp.int32).astype(F32)
        outs.append(total)
    return outs[0] if len(outs) == 1 else jnp.concatenate(outs, axis=0)


def solution(mesh):
    spec = P("groups", "ctx", "head", None)
    return jax.shard_map(
        per_device,
        mesh=mesh,
        in_specs=(spec,) * 5 + (P("groups", None, "ctx"),),
        out_specs=spec,
        check_vma=False,
    )
```
